32 devices in a mesh: dp: 4 (over y, x), fsdp: 2 (over core), ctx: 4 (over z).
Axes of the slice: x: 2, y: 2, z: 4, core: 2. Of those that a mesh axis runs over, the one named last changes fastest.
Arguments:
- tokens: bfloat16 [16384, 8192], P(('dp', 'ctx')), may hold values from -6 to 6
- grad_hidden: bfloat16 [16384, 256], P(('dp', 'ctx'), 'fsdp'), may hold values from -0.0625 to 0.0625
- master: float32 [256, 8192], P(('fsdp', 'ctx')), may hold values from -3 to 3
- first_moment: float32 [256, 8192], P(('fsdp', 'ctx')), may hold values from -2 to 2
- second_moment: float32 [256, 8192], P(('fsdp', 'ctx')), may hold values from 0.01 to 1
- clip_scale: float32 [], replicated, may hold values from 0.2 to 1
Outputs:
- new_weights: bfloat16 [256, 8192], P('fsdp')
- new_master: float32 [256, 8192], P(('fsdp', 'ctx'))
- new_first: float32 [256, 8192], P(('fsdp', 'ctx'))
- new_second: float32 [256, 8192], P(('fsdp', 'ctx'))
The draws below stay inside these ranges and needn't reach their ends.
All inputs are finite; a program needn't handle non-finite values.
Results may differ from the reference program's by a relative error of at most 0.005.
Values may be sent and summed in bfloat16 or wider, within the bound.
A program may use at most 128 MiB of HBM per device.

```python
import math
import jax
import jax.numpy as jnp
from jax import lax

D = 8192
TOK_DEV = 1024
STEP = 10
TOKENS = 16384
ROWS = 256
N_DP = 4
N_CTX = 4


def raised(result, key, source, target, parts, factor):
    owner, partner = [(jnp.arange(result.shape[dim]) // (result.shape[dim] // parts)).reshape([-1 if axis == dim else 1 for axis in range(result.ndim)]) for dim in (source, target)]
    chosen = jax.random.permutation(key, parts)[partner]
    strong = (owner == chosen) | (owner == (partner + parts // 2) % parts)
    return jnp.where(strong, factor * result, result)


def block_scale(own_key, extent, shards, least, top_value):
    def one(axis_at, shards_of):
        heights = jax.random.uniform(jax.random.fold_in(jax.random.fold_in(own_key, 6), axis_at), (shards_of,), jnp.float32, least / len(shards), top_value / len(shards))
        return jnp.repeat(jnp.exp(heights), extent[axis_at] // shards_of).reshape((-1,) + (1,) * (len(extent) - axis_at - 1))

    factor_of = one(*shards[0])
    for cut in shards[1:]:
        factor_of = factor_of * one(*cut)
    return factor_of


def normal_values(key, shape, scale, most, cuts=(), kind=jnp.bfloat16):
    drawn = jax.random.normal(key, shape, jnp.float32) * scale
    if len(cuts) > 0:
        drawn = block_scale(key, shape, cuts, -0.22, 0.18) * drawn
    return jnp.clip(drawn, min=-most, max=most).astype(kind)


def gaussian_with(key, dims, scale, most, cuts, heavy, held_as=jnp.bfloat16):
    values = scale * jax.random.normal(key, dims, jnp.float32)
    if cuts:
        values = values * block_scale(key, dims, cuts, -0.22, 0.18)
    return jnp.clip(raised(values, jax.random.fold_in(key, 3), *heavy), -most, most).astype(held_as)


def setup_inputs(seed: int = 0) -> dict:
    key_list = jax.random.split(jax.random.key(seed), 7)
    return {
        "tokens": normal_values(key_list[0], (TOKENS, D), 1.0, 6.0, ((0, 16),)),
        "grad_hidden": gaussian_with(key_list[1], (TOKENS, ROWS), TOKENS ** -0.5, 0.0625, ((0, 16), (1, 2)), (0, 1, 16, 2.0)),
        "master": normal_values(key_list[2], (ROWS, D), 0.5, 3.0, ((0, 8),), jnp.float32),
        "first_moment": normal_values(key_list[3], (ROWS, D), 0.3, 2.0, ((0, 8),), jnp.float32),
        "second_moment": jnp.clip(jnp.exp(math.log(1.0) - 4.6051702 * jax.random.uniform(key_list[4], (ROWS, D), jnp.float32) ** block_scale(key_list[4], (ROWS, D), ((0, 8),), -0.2, 0.2)), 0.01, 1.0),
        "clip_scale": jnp.clip(jax.random.uniform(key_list[5], (), jnp.float32, 0.2, 1.0), 0.2, 1.0),
    }


BETA_ONE = 0.9
BETA_TWO = 0.95
EPSILON = 1e-08
LEARNING_RATE = 0.02
DECAY = 0.1

def adamw(grad_sum, master, first_moment, second_moment, clip_scale):
    scaled = clip_scale * grad_sum
    first_new = BETA_ONE * first_moment + (1.0 - BETA_ONE) * scaled
    second_new = BETA_TWO * second_moment + (1.0 - BETA_TWO) * scaled * scaled
    first_hat = first_new / (1.0 - BETA_ONE ** STEP)
    second_hat = second_new / (1.0 - BETA_TWO ** STEP)
    update = first_hat / (jnp.sqrt(second_hat) + EPSILON)
    fresh_master = master - LEARNING_RATE * (update + DECAY * master)
    return (fresh_master, first_new, second_new)

def reference(tokens, grad_hidden, master, first_moment, second_moment, clip_scale):
    blocks = N_DP * N_CTX
    token_blocks = tokens.reshape(blocks, TOK_DEV, D)
    hidden_blocks = grad_hidden.reshape(blocks, TOK_DEV, ROWS)

    def add_block(total, blocks_pair):
        token_block, hidden_block = blocks_pair
        partial_value = jnp.dot(hidden_block.astype(jnp.float32).T, token_block.astype(jnp.float32), preferred_element_type=jnp.float32)
        partial_value = lax.optimization_barrier(partial_value.astype(jnp.bfloat16)).astype(jnp.float32)
        return (total + partial_value, None)
    grad_sum, _ = lax.scan(add_block, jnp.zeros((ROWS, D), jnp.float32), (token_blocks, hidden_blocks))
    fresh_master, first_new, second_new = adamw(grad_sum, master, first_moment, second_moment, clip_scale)
    return (fresh_master.astype(jnp.bfloat16), fresh_master, first_new, second_new)
```

```python
import contextlib
import functools

import jax
import jax.numpy as jnp
from jax import lax
from jax.experimental import pallas as pl
from jax.experimental.pallas import tpu as pltpu
from jax.sharding import PartitionSpec as P

STEP = 10


BETA_ONE = 0.9
BETA_TWO = 0.95
EPSILON = 1e-08
LEARNING_RATE = 0.02
DECAY = 0.1

CHUNKS = 16
BLOCKS = 4
LAGS = (0, 4, 7, 10, 13, 16, 20)
TRACE = False
MESH = pl.DeviceIdType.MESH


def scope(name):
    return jax.named_scope(name) if TRACE else contextlib.nullcontext()


def adamw(grad_sum, master, first_moment, second_moment, clip_scale):
    scaled = clip_scale * grad_sum
    first_new = BETA_ONE * first_moment + (1.0 - BETA_ONE) * scaled
    second_new = BETA_TWO * second_moment + (1.0 - BETA_TWO) * scaled * scaled
    first_hat = first_new / (1.0 - BETA_ONE**STEP)
    second_hat = second_new / (1.0 - BETA_TWO**STEP)
    update = first_hat / (jnp.sqrt(second_hat) + EPSILON)
    fresh_master = master - LEARNING_RATE * (update + DECAY * master)
    return (fresh_master, first_new, second_new)


def reduce_kernel(
    nc, chunks,
    clip_ref, grad_hbm, tok_hbm, master_hbm, first_hbm, second_hbm,
    gathered,
    grad, columns, tok, state,
    part, part_recv, half_send, half_recv, mid, mid_recv, weights,
    grad_sem, tok_sem, state_sem,
    part_ss, part_rs, half_ss, half_rs, mid_ss, mid_rs, near_ss, near_rs,
    own_ss, pass_ss, one_rs, two_rs, far_rs,
):
    d = lax.axis_index("dp")
    c = lax.axis_index("ctx")
    x = lax.rem(d, 2)
    y = d // 2
    x_peer = d + 1 - 2 * x
    y_peer = d + 2 - 4 * y
    row_dev, width = weights.shape[1:]
    wide = 4 * width
    bf16, f32 = jnp.bfloat16, jnp.float32

    def place(k):
        odd = lax.rem(k, 2)
        one = x + odd * (y - x)
        two = y + odd * (x - y)
        one_peer = x_peer + odd * (y_peer - x_peer)
        two_peer = y_peer + odd * (x_peer - y_peer)
        return one, two, one_peer, two_peer

    def wide_cols(k):
        return pl.ds(pl.multiple_of(k * wide, 128), wide)

    def cols(k, s):
        return pl.ds(pl.multiple_of(k * wide + s * width, 128), width)

    def tok_copy(k):
        return pltpu.make_async_copy(tok_hbm.at[:, wide_cols(k)], tok.at[:, wide_cols(k)], tok_sem.at[k])

    def state_copies(k):
        one, two, _, _ = place(k)
        return [
            pltpu.make_async_copy(src.at[:, cols(k, 2 * one + two)], state.at[k, i], state_sem.at[k, i])
            for i, src in enumerate((master_hbm, first_hbm, second_hbm))
        ]

    def block(k, s):
        return gathered.at[:, :, cols(k, s)]

    def send(src, dst, ss, rs, axis, target):
        pltpu.make_async_remote_copy(
            src_ref=src, dst_ref=dst, send_sem=ss, recv_sem=rs,
            device_id={axis: target}, device_id_type=MESH,
        ).start()

    def take(like, sem):
        pltpu.make_async_copy(like, like, sem).wait()

    grad_copy = pltpu.make_async_copy(grad_hbm, grad, grad_sem)
    grad_copy.start()

    @pl.loop(0, chunks)
    def _(k):
        tok_copy(k).start()

    @pl.loop(0, chunks)
    def _(k):
        for copy in state_copies(k):
            copy.start()

    barrier = pltpu.get_barrier_semaphore()
    for peer in (x_peer, y_peer):
        pl.semaphore_signal(barrier, inc=1, device_id={"dp": peer}, device_id_type=MESH)
    for j in range(1, nc):
        pl.semaphore_signal(
            barrier, inc=1, device_id={"ctx": lax.rem(c + j, nc)}, device_id_type=MESH
        )
    with scope("grad"):
        grad_copy.wait()
        columns[...] = grad[...].T
    with scope("barrier"):
        pl.semaphore_wait(barrier, nc + 1)

    def multiply(k):
        one, two, one_peer, _ = place(k)
        with scope("tokwait"):
            tok_copy(k).wait()
        with scope("matmul"):
            partial = jnp.dot(columns[...], tok[:, wide_cols(k)], preferred_element_type=f32)
            for s in range(4):
                part[k, s // 2, s % 2] = (
                    partial[:, s * width:(s + 1) * width].reshape(nc, row_dev, width).astype(bf16)
                )
        send(part.at[k, 1 - one], part_recv.at[k], part_ss.at[k], part_rs.at[k], "dp", one_peer)

    def fold_one(k):
        one, two, _, two_peer = place(k)
        with scope("wait1"):
            take(part_recv.at[k], part_rs.at[k])
        with scope("fold1"):
            half_send[k] = (
                part[k, one, 1 - two].astype(f32) + part_recv[k, 1 - two].astype(f32)
            ).astype(bf16)
        send(half_send.at[k], half_recv.at[k], half_ss.at[k], half_rs.at[k], "dp", two_peer)

    def fold_two(k):
        one, two, _, _ = place(k)
        with scope("wait2"):
            take(half_recv.at[k], half_rs.at[k])
        with scope("fold2"):
            mid[k] = (
                part[k, one, two].astype(f32) + part_recv[k, two].astype(f32)
                + half_recv[k].astype(f32)
            ).astype(bf16)
        for j in range(1, nc):
            to = lax.rem(c + j, nc)
            send(mid.at[k, to], mid_recv.at[k, j - 1], mid_ss.at[k], mid_rs.at[k], "ctx", to)

    def update(k):
        one, two, _, _ = place(k)
        s = 2 * one + two
        with scope("wait3"):
            take(mid_recv.at[k], mid_rs.at[k])
        for copy in state_copies(k):
            copy.wait()
        with scope("update"):
            total = mid[k, c].astype(f32)
            for j in range(nc - 1):
                total = total + mid_recv[k, j].astype(f32)
            rounded = total.astype(bf16)
            gathered[c, :, cols(k, s)] = rounded
            fresh, _, _ = adamw(
                rounded.astype(f32), state[k, 0], state[k, 1], state[k, 2], clip_ref[0]
            )
            weights[k] = fresh.astype(bf16)
        for j in range(1, nc):
            send(
                weights.at[k], gathered.at[c, :, cols(k, s)], near_ss.at[k], near_rs.at[k],
                "ctx", lax.rem(c + j, nc),
            )

    def share(k):
        one, two, one_peer, two_peer = place(k)
        s = 2 * one + two
        with scope("wait4"):
            take(mid_recv.at[k], near_rs.at[k])
        send(block(k, s), block(k, s), own_ss.at[k], one_rs.at[k], "dp", one_peer)
        send(block(k, s), block(k, s), own_ss.at[k], two_rs.at[k], "dp", two_peer)

    def forward(k):
        one, two, _, two_peer = place(k)
        s = 2 * (1 - one) + two
        with scope("wait5"):
            take(block(k, s), one_rs.at[k])
        send(block(k, s), block(k, s), pass_ss.at[k], far_rs.at[k], "dp", two_peer)

    def settle(k):
        with scope("wait6"):
            take(block(k, 0), two_rs.at[k])
            take(block(k, 0), far_rs.at[k])

    stages = (multiply, fold_one, fold_two, update, share, forward, settle)

    @pl.loop(0, chunks + LAGS[-1])
    def _(t):
        for stage, lag in zip(stages, LAGS):
            @pl.when(jnp.logical_and(t >= lag, t < chunks + lag))
            def _():
                stage(t - lag)

    with scope("drain"):
        @pl.loop(0, chunks)
        def _(k):
            take(part_recv.at[k], part_ss.at[k])
            take(half_recv.at[k], half_ss.at[k])
            take(mid_recv.at[k], mid_ss.at[k])
            take(mid_recv.at[k], near_ss.at[k])
            take(gathered.at[:, :, pl.ds(0, 2 * width)], own_ss.at[k])
            take(block(k, 0), pass_ss.at[k])


def apply_kernel(
    nc, blocks,
    clip_ref, gathered, master, first, second,
    weight_out, master_out, first_out, second_out,
    fresh, rounded,
    out_sem, move_sem,
):
    c = lax.axis_index("ctx")
    row_dev, dim = master.shape
    width = dim // blocks
    targets = (master_out, first_out, second_out)

    def cols(k):
        return pl.ds(pl.multiple_of(k * width, 128), width)

    def stores(k):
        return [
            pltpu.make_async_copy(fresh.at[i, :, cols(k)], dst.at[:, cols(k)], out_sem.at[k, i])
            for i, dst in enumerate(targets)
        ] + [
            pltpu.make_async_copy(
                rounded.at[:, cols(k)], weight_out.at[c, :, cols(k)], out_sem.at[k, 3]
            )
        ]

    def move(j):
        row = lax.rem(c + j, nc)
        return pltpu.make_async_copy(gathered.at[row], weight_out.at[row], move_sem.at[j - 1])

    @pl.loop(1, nc)
    def _(j):
        move(j).start()

    @pl.loop(0, blocks)
    def _(k):
        results = adamw(
            gathered[c, :, cols(k)].astype(jnp.float32),
            master[:, cols(k)], first[:, cols(k)], second[:, cols(k)], clip_ref[0],
        )
        for i, value in enumerate(results):
            fresh[i, :, cols(k)] = value
        rounded[:, cols(k)] = results[0].astype(jnp.bfloat16)
        for copy in stores(k):
            copy.start()

    @pl.loop(0, blocks)
    def _(k):
        for copy in stores(k):
            copy.wait()

    @pl.loop(1, nc)
    def _(j):
        move(j).wait()


def per_device(tokens, grad_hidden, master, first_moment, second_moment, clip_scale):
    nc = lax.axis_size("ctx")
    row_dev, dim = master.shape
    tok_rows, rows = grad_hidden.shape
    width = dim // CHUNKS // 4
    bf16, f32 = jnp.bfloat16, jnp.float32
    dma = pltpu.SemaphoreType.DMA
    hbm = pl.BlockSpec(memory_space=pl.ANY)
    smem = pl.BlockSpec(memory_space=pltpu.SMEM)
    vmem = pl.BlockSpec(memory_space=pltpu.VMEM)

    def in_vmem(a):
        return pltpu.with_memory_space_constraint(a, pltpu.VMEM)

    clip = clip_scale.reshape(1)
    gathered = pl.pallas_call(
        functools.partial(reduce_kernel, nc, CHUNKS),
        out_shape=pltpu.VMEM((nc, row_dev, dim), bf16),
        in_specs=[smem] + [hbm] * 5,
        out_specs=pl.BlockSpec(memory_space=pltpu.VMEM),
        scratch_shapes=[
            pltpu.VMEM((tok_rows, rows), bf16),
            pltpu.VMEM((rows, tok_rows), bf16),
            pltpu.VMEM((tok_rows, dim), bf16),
            pltpu.VMEM((CHUNKS, 3, row_dev, width), f32),
            pltpu.VMEM((CHUNKS, 2, 2, nc, row_dev, width), bf16),
            pltpu.VMEM((CHUNKS, 2, nc, row_dev, width), bf16),
            pltpu.VMEM((CHUNKS, nc, row_dev, width), bf16),
            pltpu.VMEM((CHUNKS, nc, row_dev, width), bf16),
            pltpu.VMEM((CHUNKS, nc, row_dev, width), bf16),
            pltpu.VMEM((CHUNKS, nc - 1, row_dev, width), bf16),
            pltpu.VMEM((CHUNKS, row_dev, width), bf16),
            dma, dma((CHUNKS,)), dma((CHUNKS, 3)),
        ] + [dma((CHUNKS,))] * 13,
        compiler_params=pltpu.CompilerParams(
            collective_id=0, has_side_effects=True, vmem_limit_bytes=48 << 20
        ),
        cost_estimate=pl.CostEstimate(
            flops=2 * rows * tok_rows * dim,
            bytes_accessed=2 * tok_rows * dim + 4 * rows * dim,
            transcendentals=0,
        ),
    )(clip, grad_hidden, tokens, master, first_moment, second_moment)
    new_weights, new_master, new_first, new_second = pl.pallas_call(
        functools.partial(apply_kernel, nc, BLOCKS),
        out_shape=(jax.ShapeDtypeStruct((nc, row_dev, dim), bf16),)
        + (jax.ShapeDtypeStruct((row_dev, dim), f32),) * 3,
        in_specs=[smem] + [vmem] * 4,
        out_specs=(hbm,) * 4,
        scratch_shapes=[
            pltpu.VMEM((3, row_dev, dim), f32),
            pltpu.VMEM((row_dev, dim), bf16),
            dma((BLOCKS, 4)), dma((nc - 1,)),
        ],
        compiler_params=pltpu.CompilerParams(vmem_limit_bytes=24 << 20),
        cost_estimate=pl.CostEstimate(
            flops=20 * row_dev * dim, bytes_accessed=40 * row_dev * dim, transcendentals=row_dev * dim
        ),
    )(clip, *(in_vmem(a) for a in (gathered, master, first_moment, second_moment)))
    return (new_weights.reshape(rows, dim), new_master, new_first, new_second)


def solution(mesh):
    in_specs = (
        P(("dp", "ctx"), None),
        P(("dp", "ctx"), "fsdp"),
        P(("fsdp", "ctx"), None),
        P(("fsdp", "ctx"), None),
        P(("fsdp", "ctx"), None),
        P(),
    )
    out_specs = (
        P("fsdp", None),
        P(("fsdp", "ctx"), None),
        P(("fsdp", "ctx"), None),
        P(("fsdp", "ctx"), None),
    )
    return jax.shard_map(
        per_device, mesh=mesh, in_specs=in_specs, out_specs=out_specs, check_vma=False
    )
```

```python
import functools

import jax
import jax.numpy as jnp
from jax import lax
from jax.experimental import pallas as pl
from jax.experimental.pallas import tpu as pltpu
from jax.sharding import PartitionSpec as P

STEP = 10


BETA_ONE = 0.9
BETA_TWO = 0.95
EPSILON = 1e-08
LEARNING_RATE = 0.02
DECAY = 0.1

CHUNKS = 16
BLOCKS = 4
REDUCE = 'NNNNNZNNZNNNNNNN'
GATHER = 'NNNNNGGNNNNDNNND'
ORDER = (
    0, 1, 2, 3, 4, 5, 6, 7, 16, 17, 8, 18, 9, 19, 23, 20,
    10, 32, 22, 11, 34, 12, 33, 13, 35, 36, 24, 21, 39, 38, 14, 48,
    15, 50, 27, 26, 49, 40, 25, 29, 51, 37, 52, 30, 55, 28, 31, 43,
    64, 56, 42, 54, 66, 45, 65, 41, 67, 46, 53, 71, 68, 44, 59, 82,
    72, 70, 47, 58, 80, 61, 81, 69, 57, 87, 84, 62, 83, 88, 60, 75,
    63, 86, 74, 77, 73, 78, 98, 91, 85, 97, 76, 90, 79, 93, 99, 94,
    89, 92, 96, 104, 100, 106, 107, 103, 102, 109, 95, 110, 105, 111, 101, 108,
)
MESH = pl.DeviceIdType.MESH


def adamw(grad_sum, master, first_moment, second_moment, clip_scale):
    scaled = clip_scale * grad_sum
    first_new = BETA_ONE * first_moment + (1.0 - BETA_ONE) * scaled
    second_new = BETA_TWO * second_moment + (1.0 - BETA_TWO) * scaled * scaled
    first_hat = first_new / (1.0 - BETA_ONE**STEP)
    second_hat = second_new / (1.0 - BETA_TWO**STEP)
    update = first_hat / (jnp.sqrt(second_hat) + EPSILON)
    fresh_master = master - LEARNING_RATE * (update + DECAY * master)
    return (fresh_master, first_new, second_new)


def reduce_kernel(
    nc, chunks,
    clip_ref, grad_hbm, tok_hbm, master_hbm, first_hbm, second_hbm,
    gathered, master, first, second,
    grad, columns, tok,
    part, part_recv, half_send, half_recv, mid, mid_recv, weights,
    cross_recv, cross_sum, pair_send, pair_recv, quarter_send, quarter_recv, wide_weights,
    grad_sem, tok_sem, state_sem,
    part_ss, part_rs, half_ss, half_rs, mid_ss, mid_rs, near_ss, near_rs,
    own_ss, pass_ss, one_rs, two_rs, far_rs,
):
    d = lax.axis_index("dp")
    c = lax.axis_index("ctx")
    x = lax.rem(d, 2)
    y = d // 2
    x_peer = d + 1 - 2 * x
    y_peer = d + 2 - 4 * y
    far_peer = 3 - d
    row_dev, width = weights.shape[1:]
    wide = 4 * width
    crossed = [k for k in range(chunks) if REDUCE[k] == "Z"]
    widened = [k for k in range(chunks) if GATHER[k] == "G"]
    bf16, f32 = jnp.bfloat16, jnp.float32

    def place(k):
        return (y, x, y_peer, x_peer) if k % 2 else (x, y, x_peer, y_peer)

    def wide_cols(k):
        return pl.ds(pl.multiple_of(k * wide, 128), wide)

    def cols(k, s):
        return pl.ds(pl.multiple_of(k * wide + s * width, 128), width)

    def tok_copy(k):
        return pltpu.make_async_copy(tok_hbm.at[:, wide_cols(k)], tok.at[:, wide_cols(k)], tok_sem.at[k])

    state_copies = [
        pltpu.make_async_copy(src, dst, state_sem.at[i])
        for i, (src, dst) in enumerate(
            ((master_hbm, master), (first_hbm, first), (second_hbm, second))
        )
    ]

    def block(k, s):
        return gathered.at[:, :, cols(k, s)]

    def send(src, dst, ss, rs, axis, target):
        pltpu.make_async_remote_copy(
            src_ref=src, dst_ref=dst, send_sem=ss, recv_sem=rs,
            device_id={axis: target}, device_id_type=MESH,
        ).start()

    def take(like, sem):
        pltpu.make_async_copy(like, like, sem).wait()

    grad_copy = pltpu.make_async_copy(grad_hbm, grad, grad_sem)
    grad_copy.start()

    @pl.loop(0, chunks)
    def _(k):
        tok_copy(k).start()

    for copy in state_copies:
        copy.start()

    barrier = pltpu.get_barrier_semaphore()
    for peer in (x_peer, y_peer, far_peer):
        pl.semaphore_signal(barrier, inc=1, device_id={"dp": peer}, device_id_type=MESH)
    for j in range(1, nc):
        pl.semaphore_signal(
            barrier, inc=1, device_id={"ctx": lax.rem(c + j, nc)}, device_id_type=MESH
        )
    grad_copy.wait()
    columns[...] = grad[...].T
    pl.semaphore_wait(barrier, nc + 2)

    def others():
        return [lax.rem(c + j, nc) for j in range(1, nc)]

    def multiply(k):
        one, two, one_peer, _ = place(k)
        tok_copy(k).wait()
        partial = jnp.dot(columns[...], tok[:, wide_cols(k)], preferred_element_type=f32)
        for s in range(4):
            part[k, s // 2, s % 2] = (
                partial[:, s * width:(s + 1) * width].reshape(nc, row_dev, width).astype(bf16)
            )
        if REDUCE[k] == "N":
            send(part.at[k, 1 - one], part_recv.at[k], part_ss.at[k], part_rs.at[k], "dp", one_peer)
        else:
            z = crossed.index(k)
            for j, to in enumerate(others()):
                send(
                    part.at[k, :, :, to], cross_recv.at[z, j], part_ss.at[k], part_rs.at[k], "ctx", to
                )

    def fold_one(k):
        one, two, one_peer, two_peer = place(k)
        if REDUCE[k] == "N":
            take(part_recv.at[k], part_rs.at[k])
            half_send[k] = (
                part[k, one, 1 - two].astype(f32) + part_recv[k, 1 - two].astype(f32)
            ).astype(bf16)
            send(half_send.at[k], half_recv.at[k], half_ss.at[k], half_rs.at[k], "dp", two_peer)
        else:
            z = crossed.index(k)
            take(cross_recv.at[z], part_rs.at[k])
            total = part[k, :, :, c].astype(f32)
            for j in range(nc - 1):
                total = total + cross_recv[z, j].astype(f32)
            cross_sum[z] = total
            pair_send[z] = cross_sum[z, 1 - one].astype(bf16)
            send(pair_send.at[z], pair_recv.at[z], half_ss.at[k], half_rs.at[k], "dp", one_peer)

    def fold_two(k):
        one, two, _, two_peer = place(k)
        if REDUCE[k] == "N":
            take(half_recv.at[k], half_rs.at[k])
            mid[k] = (
                part[k, one, two].astype(f32) + part_recv[k, two].astype(f32)
                + half_recv[k].astype(f32)
            ).astype(bf16)
            for j, to in enumerate(others()):
                send(mid.at[k, to], mid_recv.at[k, j], mid_ss.at[k], mid_rs.at[k], "ctx", to)
        else:
            z = crossed.index(k)
            take(pair_recv.at[z], half_rs.at[k])
            quarter_send[z] = (
                cross_sum[z, one, 1 - two] + pair_recv[z, 1 - two].astype(f32)
            ).astype(bf16)
            send(quarter_send.at[z], quarter_recv.at[z], mid_ss.at[k], mid_rs.at[k], "dp", two_peer)

    def update(k):
        one, two, one_peer, two_peer = place(k)
        here = cols(k, 2 * one + two)
        if REDUCE[k] == "N":
            take(mid_recv.at[k], mid_rs.at[k])
            total = mid[k, c].astype(f32)
            for j in range(nc - 1):
                total = total + mid_recv[k, j].astype(f32)
        else:
            z = crossed.index(k)
            take(quarter_recv.at[z], mid_rs.at[k])
            total = (
                cross_sum[z, one, two] + pair_recv[z, two].astype(f32) + quarter_recv[z].astype(f32)
            )
        rounded = total.astype(bf16)
        gathered[c, :, here] = rounded
        if GATHER[k] == "G":
            piece = gathered.at[c, :, here]
            send(piece, piece, own_ss.at[k], one_rs.at[k], "dp", one_peer)
            send(piece, piece, own_ss.at[k], two_rs.at[k], "dp", two_peer)
        else:
            fresh, _, _ = adamw(
                rounded.astype(f32), master[:, here], first[:, here], second[:, here], clip_ref[0]
            )
            weights[k] = fresh.astype(bf16)
            for to in others():
                send(
                    weights.at[k], gathered.at[c, :, here], near_ss.at[k], near_rs.at[k], "ctx", to
                )

    def share(k):
        one, two, one_peer, two_peer = place(k)
        s = 2 * one + two
        if GATHER[k] == "G":
            piece = gathered.at[c, :, cols(k, 2 * (1 - one) + two)]
            take(piece, one_rs.at[k])
            send(piece, piece, pass_ss.at[k], far_rs.at[k], "dp", two_peer)
        else:
            take(mid_recv.at[k], near_rs.at[k])
            send(block(k, s), block(k, s), own_ss.at[k], one_rs.at[k], "dp", one_peer)
            send(block(k, s), block(k, s), own_ss.at[k], two_rs.at[k], "dp", two_peer)
            if GATHER[k] == "D":
                send(block(k, s), block(k, s), own_ss.at[k], far_rs.at[k], "dp", far_peer)

    def forward(k):
        one, two, _, two_peer = place(k)
        if GATHER[k] == "G":
            g = widened.index(k)
            piece = weights.at[k]
            take(piece, two_rs.at[k])
            take(piece, far_rs.at[k])
            here = wide_cols(k)
            fresh, _, _ = adamw(
                gathered[c, :, here].astype(f32),
                master[:, here], first[:, here], second[:, here], clip_ref[0],
            )
            wide_weights[g] = fresh.astype(bf16)
            for to in others():
                send(
                    wide_weights.at[g], gathered.at[c, :, here], near_ss.at[k], near_rs.at[k],
                    "ctx", to,
                )
        elif GATHER[k] == "N":
            s = 2 * (1 - one) + two
            take(block(k, s), one_rs.at[k])
            send(block(k, s), block(k, s), pass_ss.at[k], far_rs.at[k], "dp", two_peer)

    def wide_take(k, sem):
        take(gathered.at[pl.ds(0, nc - 1), :, wide_cols(k)], sem)

    def settle(k):
        if GATHER[k] == "G":
            wide_take(k, near_rs.at[k])
        else:
            if GATHER[k] == "D":
                take(block(k, 0), one_rs.at[k])
            take(block(k, 0), two_rs.at[k])
            take(block(k, 0), far_rs.at[k])

    stages = (multiply, fold_one, fold_two, update, share, forward, settle)
    ready = False
    for entry in ORDER:
        stage, k = divmod(entry, chunks)
        if stage == 3 and not ready:
            for copy in state_copies:
                copy.wait()
            ready = True
        stages[stage](k)

    for k in range(chunks):
        if REDUCE[k] == "N":
            take(part_recv.at[k], part_ss.at[k])
            take(half_recv.at[k], half_ss.at[k])
            take(mid_recv.at[k], mid_ss.at[k])
        else:
            z = crossed.index(k)
            take(cross_recv.at[z], part_ss.at[k])
            take(pair_recv.at[z], half_ss.at[k])
            take(quarter_recv.at[z], mid_ss.at[k])
        if GATHER[k] == "G":
            take(weights.at[pl.ds(0, 2)], own_ss.at[k])
            take(weights.at[k], pass_ss.at[k])
            wide_take(k, near_ss.at[k])
        else:
            take(mid_recv.at[k], near_ss.at[k])
            copies = 3 if GATHER[k] == "D" else 2
            take(gathered.at[:, :, pl.ds(0, copies * width)], own_ss.at[k])
            if GATHER[k] == "N":
                take(block(k, 0), pass_ss.at[k])


def apply_kernel(
    nc, blocks,
    clip_ref, gathered, master, first, second,
    weight_out, master_out, first_out, second_out,
    fresh, rounded,
    out_sem, move_sem,
):
    c = lax.axis_index("ctx")
    row_dev, dim = master.shape
    width = dim // blocks
    targets = (master_out, first_out, second_out)

    def cols(k):
        return pl.ds(pl.multiple_of(k * width, 128), width)

    def stores(k):
        return [
            pltpu.make_async_copy(fresh.at[i, :, cols(k)], dst.at[:, cols(k)], out_sem.at[k, i])
            for i, dst in enumerate(targets)
        ] + [
            pltpu.make_async_copy(
                rounded.at[:, cols(k)], weight_out.at[c, :, cols(k)], out_sem.at[k, 3]
            )
        ]

    def move(j):
        row = lax.rem(c + j, nc)
        return pltpu.make_async_copy(gathered.at[row], weight_out.at[row], move_sem.at[j - 1])

    @pl.loop(1, nc)
    def _(j):
        move(j).start()

    @pl.loop(0, blocks)
    def _(k):
        results = adamw(
            gathered[c, :, cols(k)].astype(jnp.float32),
            master[:, cols(k)], first[:, cols(k)], second[:, cols(k)], clip_ref[0],
        )
        for i, value in enumerate(results):
            fresh[i, :, cols(k)] = value
        rounded[:, cols(k)] = results[0].astype(jnp.bfloat16)
        for copy in stores(k):
            copy.start()

    @pl.loop(0, blocks)
    def _(k):
        for copy in stores(k):
            copy.wait()

    @pl.loop(1, nc)
    def _(j):
        move(j).wait()


def per_device(tokens, grad_hidden, master, first_moment, second_moment, clip_scale):
    nc = lax.axis_size("ctx")
    row_dev, dim = master.shape
    tok_rows, rows = grad_hidden.shape
    width = dim // CHUNKS // 4
    crossed = max(1, REDUCE.count("Z"))
    widened = max(1, GATHER.count("G"))
    bf16, f32 = jnp.bfloat16, jnp.float32
    dma = pltpu.SemaphoreType.DMA
    hbm = pl.BlockSpec(memory_space=pl.ANY)
    smem = pl.BlockSpec(memory_space=pltpu.SMEM)
    vmem = pl.BlockSpec(memory_space=pltpu.VMEM)

    def in_hbm(a):
        return pltpu.with_memory_space_constraint(a, pltpu.HBM)

    def in_vmem(a):
        return pltpu.with_memory_space_constraint(a, pltpu.VMEM)

    clip = clip_scale.reshape(1)
    kept = pl.pallas_call(
        functools.partial(reduce_kernel, nc, CHUNKS),
        out_shape=(pltpu.VMEM((nc, row_dev, dim), bf16),) + (pltpu.VMEM((row_dev, dim), f32),) * 3,
        in_specs=[smem] + [hbm] * 5,
        out_specs=(vmem,) * 4,
        scratch_shapes=[
            pltpu.VMEM((tok_rows, rows), bf16),
            pltpu.VMEM((rows, tok_rows), bf16),
            pltpu.VMEM((tok_rows, dim), bf16),
            pltpu.VMEM((CHUNKS, 2, 2, nc, row_dev, width), bf16),
            pltpu.VMEM((CHUNKS, 2, nc, row_dev, width), bf16),
            pltpu.VMEM((CHUNKS, nc, row_dev, width), bf16),
            pltpu.VMEM((CHUNKS, nc, row_dev, width), bf16),
            pltpu.VMEM((CHUNKS, nc, row_dev, width), bf16),
            pltpu.VMEM((CHUNKS, nc - 1, row_dev, width), bf16),
            pltpu.VMEM((CHUNKS, row_dev, width), bf16),
            pltpu.VMEM((crossed, nc - 1, 2, 2, row_dev, width), bf16),
            pltpu.VMEM((crossed, 2, 2, row_dev, width), f32),
            pltpu.VMEM((crossed, 2, row_dev, width), bf16),
            pltpu.VMEM((crossed, 2, row_dev, width), bf16),
            pltpu.VMEM((crossed, row_dev, width), bf16),
            pltpu.VMEM((crossed, row_dev, width), bf16),
            pltpu.VMEM((widened, row_dev, 4 * width), bf16),
            dma, dma((CHUNKS,)), dma((3,)),
        ] + [dma((CHUNKS,))] * 13,
        compiler_params=pltpu.CompilerParams(
            collective_id=0, has_side_effects=True, vmem_limit_bytes=48 << 20
        ),
        cost_estimate=pl.CostEstimate(
            flops=2 * rows * tok_rows * dim,
            bytes_accessed=2 * tok_rows * dim + 4 * rows * dim,
            transcendentals=0,
        ),
    )(clip, *(in_hbm(a) for a in (grad_hidden, tokens, master, first_moment, second_moment)))
    new_weights, new_master, new_first, new_second = pl.pallas_call(
        functools.partial(apply_kernel, nc, BLOCKS),
        out_shape=(jax.ShapeDtypeStruct((nc, row_dev, dim), bf16),)
        + (jax.ShapeDtypeStruct((row_dev, dim), f32),) * 3,
        in_specs=[smem] + [vmem] * 4,
        out_specs=(hbm,) * 4,
        scratch_shapes=[
            pltpu.VMEM((3, row_dev, dim), f32),
            pltpu.VMEM((row_dev, dim), bf16),
            dma((BLOCKS, 4)), dma((nc - 1,)),
        ],
        compiler_params=pltpu.CompilerParams(vmem_limit_bytes=24 << 20),
        cost_estimate=pl.CostEstimate(
            flops=20 * row_dev * dim, bytes_accessed=40 * row_dev * dim, transcendentals=row_dev * dim
        ),
    )(clip, *(in_vmem(a) for a in kept))
    return (new_weights.reshape(rows, dim), new_master, new_first, new_second)


def solution(mesh):
    in_specs = (
        P(("dp", "ctx"), None),
        P(("dp", "ctx"), "fsdp"),
        P(("fsdp", "ctx"), None),
        P(("fsdp", "ctx"), None),
        P(("fsdp", "ctx"), None),
        P(),
    )
    out_specs = (
        P("fsdp", None),
        P(("fsdp", "ctx"), None),
        P(("fsdp", "ctx"), None),
        P(("fsdp", "ctx"), None),
    )
    return jax.shard_map(
        per_device, mesh=mesh, in_specs=in_specs, out_specs=out_specs, check_vma=False
    )
```

```python
import functools

import jax
import jax.numpy as jnp
from jax import lax
from jax.experimental import pallas as pl
from jax.experimental.pallas import tpu as pltpu
from jax.sharding import PartitionSpec as P

STEP = 10


BETA_ONE = 0.9
BETA_TWO = 0.95
EPSILON = 1e-08
LEARNING_RATE = 0.02
DECAY = 0.1

CHUNKS = 16
BLOCKS = 4
REDUCE = 'NNNNZNNZHHHNNNNN'
GATHER = 'NNNNPNNDGNNGNNDN'
ORDER = (
    0, 1, 2, 3, 4, 5, 6, 16, 17, 7, 8, 18, 9, 19, 22, 21,
    10, 32, 11, 20, 33, 34, 12, 24, 13, 35, 25, 37, 14, 38, 15, 23,
    64, 65, 36, 26, 40, 27, 66, 28, 67, 29, 41, 69, 70, 31, 30, 39,
    68, 96, 56, 43, 97, 42, 44, 98, 57, 45, 99, 47, 71, 101, 72, 84,
    102, 58, 46, 75, 114, 113, 112, 73, 76, 115, 77, 117, 104, 100, 79, 118,
    103, 74, 107, 129, 78, 105, 120, 108, 109, 111, 106, 123, 133, 110, 134, 124,
    121, 116, 125, 130, 127, 122, 131, 136, 142, 140, 128, 137, 141, 132, 135, 139,
    143, 138,
)
MESH = pl.DeviceIdType.MESH


def adamw(grad_sum, master, first_moment, second_moment, clip_scale):
    scaled = clip_scale * grad_sum
    first_new = BETA_ONE * first_moment + (1.0 - BETA_ONE) * scaled
    second_new = BETA_TWO * second_moment + (1.0 - BETA_TWO) * scaled * scaled
    first_hat = first_new / (1.0 - BETA_ONE**STEP)
    second_hat = second_new / (1.0 - BETA_TWO**STEP)
    update = first_hat / (jnp.sqrt(second_hat) + EPSILON)
    fresh_master = master - LEARNING_RATE * (update + DECAY * master)
    return (fresh_master, first_new, second_new)


def reduce_kernel(
    nc, chunks,
    clip_ref, grad_hbm, tok_hbm, master_hbm, first_hbm, second_hbm,
    gathered, master, first, second,
    grad, columns, tok,
    part, part_recv, half_send, half_recv, mid, mid_recv, weights,
    cross_recv, cross_sum, pair_send, pair_recv, quarter_send, quarter_recv, wide_weights, folded,
    grad_sem, tok_sem, state_sem,
    part_ss, part_rs, half_ss, half_rs, mid_ss, mid_rs, near_ss, near_rs,
    own_ss, pass_ss, one_rs, two_rs, far_rs,
    cross_ss, cross_rs, pair_ss, pair_rs,
):
    d = lax.axis_index("dp")
    c = lax.axis_index("ctx")
    x = lax.rem(d, 2)
    y = d // 2
    x_peer = d + 1 - 2 * x
    y_peer = d + 2 - 4 * y
    far_peer = 3 - d
    row_dev, width = weights.shape[1:]
    wide = 4 * width
    half = nc // 2
    hi, lo = c // 2, lax.rem(c, 2)
    pair = c + 1 - 2 * lo
    crossed = [k for k in range(chunks) if REDUCE[k] == "Z"]
    widened = [k for k in range(chunks) if GATHER[k] == "G"]
    bf16, f32 = jnp.bfloat16, jnp.float32

    def place(k):
        return (y, x, y_peer, x_peer) if k % 2 else (x, y, x_peer, y_peer)

    def wide_cols(k):
        return pl.ds(pl.multiple_of(k * wide, 128), wide)

    def cols(k, s):
        return pl.ds(pl.multiple_of(k * wide + s * width, 128), width)

    def tok_copy(k):
        return pltpu.make_async_copy(tok_hbm.at[:, wide_cols(k)], tok.at[:, wide_cols(k)], tok_sem.at[k])

    state_copies = [
        pltpu.make_async_copy(src, dst, state_sem.at[i])
        for i, (src, dst) in enumerate(
            ((master_hbm, master), (first_hbm, first), (second_hbm, second))
        )
    ]

    def block(k, s):
        return gathered.at[:, :, cols(k, s)]

    def send(src, dst, ss, rs, axis, target):
        pltpu.make_async_remote_copy(
            src_ref=src, dst_ref=dst, send_sem=ss, recv_sem=rs,
            device_id={axis: target}, device_id_type=MESH,
        ).start()

    def take(like, sem):
        pltpu.make_async_copy(like, like, sem).wait()

    grad_copy = pltpu.make_async_copy(grad_hbm, grad, grad_sem)
    grad_copy.start()

    @pl.loop(0, chunks)
    def _(k):
        tok_copy(k).start()

    for copy in state_copies:
        copy.start()

    barrier = pltpu.get_barrier_semaphore()
    for peer in (x_peer, y_peer, far_peer):
        pl.semaphore_signal(barrier, inc=1, device_id={"dp": peer}, device_id_type=MESH)
    for j in range(1, nc):
        pl.semaphore_signal(
            barrier, inc=1, device_id={"ctx": lax.rem(c + j, nc)}, device_id_type=MESH
        )
    grad_copy.wait()
    columns[...] = grad[...].T
    pl.semaphore_wait(barrier, nc + 2)

    def others():
        return [lax.rem(c + j, nc) for j in range(1, nc)]

    def alike():
        return [lax.rem(hi + j, half) for j in range(1, half)]

    def multiply(k):
        one, two, one_peer, _ = place(k)
        tok_copy(k).wait()
        partial = jnp.dot(columns[...], tok[:, wide_cols(k)], preferred_element_type=f32)
        for s in range(4):
            part[k, s // 2, s % 2] = (
                partial[:, s * width:(s + 1) * width].reshape(nc, row_dev, width).astype(bf16)
            )
        if REDUCE[k] != "Z":
            send(part.at[k, 1 - one], part_recv.at[k], part_ss.at[k], part_rs.at[k], "dp", one_peer)
        else:
            z = crossed.index(k)
            for j, to in enumerate(others()):
                send(
                    part.at[k, :, :, to], cross_recv.at[z, j], part_ss.at[k], part_rs.at[k], "ctx", to
                )

    def fold_one(k):
        one, two, one_peer, two_peer = place(k)
        if REDUCE[k] != "Z":
            take(part_recv.at[k], part_rs.at[k])
            half_send[k] = (
                part[k, one, 1 - two].astype(f32) + part_recv[k, 1 - two].astype(f32)
            ).astype(bf16)
            send(half_send.at[k], half_recv.at[k], half_ss.at[k], half_rs.at[k], "dp", two_peer)
        else:
            z = crossed.index(k)
            take(cross_recv.at[z], part_rs.at[k])
            total = part[k, :, :, c].astype(f32)
            for j in range(nc - 1):
                total = total + cross_recv[z, j].astype(f32)
            cross_sum[z] = total
            pair_send[z] = cross_sum[z, 1 - one].astype(bf16)
            send(pair_send.at[z], pair_recv.at[z], half_ss.at[k], half_rs.at[k], "dp", one_peer)

    def fold_two(k):
        one, two, _, two_peer = place(k)
        if REDUCE[k] != "Z":
            take(half_recv.at[k], half_rs.at[k])
            mid[k] = (
                part[k, one, two].astype(f32) + part_recv[k, two].astype(f32)
                + half_recv[k].astype(f32)
            ).astype(bf16).reshape(half, 2, row_dev, width)
            if REDUCE[k] == "H":
                send(
                    mid.at[k, :, 1 - lo], mid_recv.at[k, pl.ds(0, half)],
                    mid_ss.at[k], mid_rs.at[k], "ctx", pair,
                )
            else:
                for j, to in enumerate(others()):
                    send(
                        mid.at[k, to // 2, lax.rem(to, 2)], mid_recv.at[k, j],
                        mid_ss.at[k], mid_rs.at[k], "ctx", to,
                    )
        else:
            z = crossed.index(k)
            take(pair_recv.at[z], half_rs.at[k])
            quarter_send[z] = (
                cross_sum[z, one, 1 - two] + pair_recv[z, 1 - two].astype(f32)
            ).astype(bf16)
            send(quarter_send.at[z], quarter_recv.at[z], mid_ss.at[k], mid_rs.at[k], "dp", two_peer)

    def fold_pair(k):
        take(mid_recv.at[k, pl.ds(0, half)], mid_rs.at[k])
        folded[k] = (
            mid[k, :, lo].astype(f32) + mid_recv[k, pl.ds(0, half)].astype(f32)
        ).astype(bf16)
        for j, to in enumerate(alike()):
            send(
                folded.at[k, to], mid_recv.at[k, half + j],
                cross_ss.at[k], cross_rs.at[k], "ctx", 2 * to + lo,
            )

    def update(k):
        one, two, one_peer, two_peer = place(k)
        here = cols(k, 2 * one + two)
        if REDUCE[k] == "H":
            take(mid_recv.at[k, pl.ds(half, half - 1)], cross_rs.at[k])
            total = mid[k, hi, lo].astype(f32) + mid_recv[k, hi].astype(f32)
            for j in range(half, nc - 1):
                total = total + mid_recv[k, j].astype(f32)
        elif REDUCE[k] == "N":
            take(mid_recv.at[k], mid_rs.at[k])
            total = mid[k, hi, lo].astype(f32)
            for j in range(nc - 1):
                total = total + mid_recv[k, j].astype(f32)
        else:
            z = crossed.index(k)
            take(quarter_recv.at[z], mid_rs.at[k])
            total = (
                cross_sum[z, one, two] + pair_recv[z, two].astype(f32) + quarter_recv[z].astype(f32)
            )
        rounded = total.astype(bf16)
        gathered[c, :, here] = rounded
        if GATHER[k] == "G":
            piece = gathered.at[c, :, here]
            send(piece, piece, own_ss.at[k], one_rs.at[k], "dp", one_peer)
            send(piece, piece, own_ss.at[k], two_rs.at[k], "dp", two_peer)
        else:
            fresh, _, _ = adamw(
                rounded.astype(f32), master[:, here], first[:, here], second[:, here], clip_ref[0]
            )
            weights[k] = fresh.astype(bf16)
            for to in [2 * h + lo for h in alike()] if GATHER[k] in "PQ" else others():
                send(
                    weights.at[k], gathered.at[c, :, here], near_ss.at[k], near_rs.at[k], "ctx", to
                )

    def swap_pair(k):
        one, two, _, _ = place(k)
        here = cols(k, 2 * one + two)
        take(mid_recv.at[k, pl.ds(0, half - 1)], near_rs.at[k])
        send(weights.at[k], gathered.at[c, :, here], pair_ss.at[k], pair_rs.at[k], "ctx", pair)
        for h in alike():
            piece = gathered.at[2 * h + lo, :, here]
            send(piece, piece, pair_ss.at[k], pair_rs.at[k], "ctx", pair)

    def share(k):
        one, two, one_peer, two_peer = place(k)
        s = 2 * one + two
        if GATHER[k] == "G":
            piece = gathered.at[c, :, cols(k, 2 * (1 - one) + two)]
            take(piece, one_rs.at[k])
            send(piece, piece, pass_ss.at[k], far_rs.at[k], "dp", two_peer)
        else:
            if GATHER[k] in "PQ":
                take(mid_recv.at[k, pl.ds(0, half)], pair_rs.at[k])
            else:
                take(mid_recv.at[k], near_rs.at[k])
            send(block(k, s), block(k, s), own_ss.at[k], one_rs.at[k], "dp", one_peer)
            send(block(k, s), block(k, s), own_ss.at[k], two_rs.at[k], "dp", two_peer)
            if GATHER[k] in "DQ":
                send(block(k, s), block(k, s), own_ss.at[k], far_rs.at[k], "dp", far_peer)

    def forward(k):
        one, two, _, two_peer = place(k)
        if GATHER[k] == "G":
            g = widened.index(k)
            piece = weights.at[k]
            take(piece, two_rs.at[k])
            take(piece, far_rs.at[k])
            here = wide_cols(k)
            fresh, _, _ = adamw(
                gathered[c, :, here].astype(f32),
                master[:, here], first[:, here], second[:, here], clip_ref[0],
            )
            wide_weights[g] = fresh.astype(bf16)
            for to in others():
                send(
                    wide_weights.at[g], gathered.at[c, :, here], near_ss.at[k], near_rs.at[k],
                    "ctx", to,
                )
        elif GATHER[k] in "NP":
            s = 2 * (1 - one) + two
            take(block(k, s), one_rs.at[k])
            send(block(k, s), block(k, s), pass_ss.at[k], far_rs.at[k], "dp", two_peer)

    def wide_take(k, sem):
        take(gathered.at[pl.ds(0, nc - 1), :, wide_cols(k)], sem)

    def settle(k):
        if GATHER[k] == "G":
            wide_take(k, near_rs.at[k])
        else:
            if GATHER[k] in "DQ":
                take(block(k, 0), one_rs.at[k])
            take(block(k, 0), two_rs.at[k])
            take(block(k, 0), far_rs.at[k])

    stages = (
        multiply, fold_one, fold_two, fold_pair, update, swap_pair, share, forward, settle,
    )
    ready = False
    for entry in ORDER:
        stage, k = divmod(entry, chunks)
        if stage == 4 and not ready:
            for copy in state_copies:
                copy.wait()
            ready = True
        stages[stage](k)

    for k in range(chunks):
        if REDUCE[k] != "Z":
            take(part_recv.at[k], part_ss.at[k])
            take(half_recv.at[k], half_ss.at[k])
            if REDUCE[k] == "H":
                take(mid_recv.at[k, pl.ds(0, half)], mid_ss.at[k])
                take(mid_recv.at[k, pl.ds(half, half - 1)], cross_ss.at[k])
            else:
                take(mid_recv.at[k], mid_ss.at[k])
        else:
            z = crossed.index(k)
            take(cross_recv.at[z], part_ss.at[k])
            take(pair_recv.at[z], half_ss.at[k])
            take(quarter_recv.at[z], mid_ss.at[k])
        if GATHER[k] == "G":
            take(weights.at[pl.ds(0, 2)], own_ss.at[k])
            take(weights.at[k], pass_ss.at[k])
            wide_take(k, near_ss.at[k])
        else:
            if GATHER[k] in "PQ":
                take(mid_recv.at[k, pl.ds(0, half - 1)], near_ss.at[k])
                take(mid_recv.at[k, pl.ds(0, half)], pair_ss.at[k])
            else:
                take(mid_recv.at[k], near_ss.at[k])
            copies = 3 if GATHER[k] in "DQ" else 2
            take(gathered.at[:, :, pl.ds(0, copies * width)], own_ss.at[k])
            if GATHER[k] in "NP":
                take(block(k, 0), pass_ss.at[k])


def apply_kernel(
    nc, blocks,
    clip_ref, gathered, master, first, second,
    weight_out, master_out, first_out, second_out,
    fresh, rounded,
    out_sem, move_sem,
):
    c = lax.axis_index("ctx")
    row_dev, dim = master.shape
    width = dim // blocks
    targets = (master_out, first_out, second_out)

    def cols(k):
        return pl.ds(pl.multiple_of(k * width, 128), width)

    def stores(k):
        return [
            pltpu.make_async_copy(fresh.at[i, :, cols(k)], dst.at[:, cols(k)], out_sem.at[k, i])
            for i, dst in enumerate(targets)
        ] + [
            pltpu.make_async_copy(
                rounded.at[:, cols(k)], weight_out.at[c, :, cols(k)], out_sem.at[k, 3]
            )
        ]

    def move(j):
        row = lax.rem(c + j, nc)
        return pltpu.make_async_copy(gathered.at[row], weight_out.at[row], move_sem.at[j - 1])

    @pl.loop(1, nc)
    def _(j):
        move(j).start()

    @pl.loop(0, blocks)
    def _(k):
        results = adamw(
            gathered[c, :, cols(k)].astype(jnp.float32),
            master[:, cols(k)], first[:, cols(k)], second[:, cols(k)], clip_ref[0],
        )
        for i, value in enumerate(results):
            fresh[i, :, cols(k)] = value
        rounded[:, cols(k)] = results[0].astype(jnp.bfloat16)
        for copy in stores(k):
            copy.start()

    @pl.loop(0, blocks)
    def _(k):
        for copy in stores(k):
            copy.wait()

    @pl.loop(1, nc)
    def _(j):
        move(j).wait()


def per_device(tokens, grad_hidden, master, first_moment, second_moment, clip_scale):
    nc = lax.axis_size("ctx")
    row_dev, dim = master.shape
    tok_rows, rows = grad_hidden.shape
    width = dim // CHUNKS // 4
    crossed = max(1, REDUCE.count("Z"))
    widened = max(1, GATHER.count("G"))
    bf16, f32 = jnp.bfloat16, jnp.float32
    dma = pltpu.SemaphoreType.DMA
    hbm = pl.BlockSpec(memory_space=pl.ANY)
    smem = pl.BlockSpec(memory_space=pltpu.SMEM)
    vmem = pl.BlockSpec(memory_space=pltpu.VMEM)

    def in_hbm(a):
        return pltpu.with_memory_space_constraint(a, pltpu.HBM)

    def in_vmem(a):
        return pltpu.with_memory_space_constraint(a, pltpu.VMEM)

    clip = clip_scale.reshape(1)
    kept = pl.pallas_call(
        functools.partial(reduce_kernel, nc, CHUNKS),
        out_shape=(pltpu.VMEM((nc, row_dev, dim), bf16),) + (pltpu.VMEM((row_dev, dim), f32),) * 3,
        in_specs=[smem] + [hbm] * 5,
        out_specs=(vmem,) * 4,
        scratch_shapes=[
            pltpu.VMEM((tok_rows, rows), bf16),
            pltpu.VMEM((rows, tok_rows), bf16),
            pltpu.VMEM((tok_rows, dim), bf16),
            pltpu.VMEM((CHUNKS, 2, 2, nc, row_dev, width), bf16),
            pltpu.VMEM((CHUNKS, 2, nc, row_dev, width), bf16),
            pltpu.VMEM((CHUNKS, nc, row_dev, width), bf16),
            pltpu.VMEM((CHUNKS, nc, row_dev, width), bf16),
            pltpu.VMEM((CHUNKS, nc // 2, 2, row_dev, width), bf16),
            pltpu.VMEM((CHUNKS, nc - 1, row_dev, width), bf16),
            pltpu.VMEM((CHUNKS, row_dev, width), bf16),
            pltpu.VMEM((crossed, nc - 1, 2, 2, row_dev, width), bf16),
            pltpu.VMEM((crossed, 2, 2, row_dev, width), f32),
            pltpu.VMEM((crossed, 2, row_dev, width), bf16),
            pltpu.VMEM((crossed, 2, row_dev, width), bf16),
            pltpu.VMEM((crossed, row_dev, width), bf16),
            pltpu.VMEM((crossed, row_dev, width), bf16),
            pltpu.VMEM((widened, row_dev, 4 * width), bf16),
            pltpu.VMEM((CHUNKS, nc // 2, row_dev, width), bf16),
            dma, dma((CHUNKS,)), dma((3,)),
        ] + [dma((CHUNKS,))] * 17,
        compiler_params=pltpu.CompilerParams(
            collective_id=0, has_side_effects=True, vmem_limit_bytes=48 << 20
        ),
        cost_estimate=pl.CostEstimate(
            flops=2 * rows * tok_rows * dim,
            bytes_accessed=2 * tok_rows * dim + 4 * rows * dim,
            transcendentals=0,
        ),
    )(clip, *(in_hbm(a) for a in (grad_hidden, tokens, master, first_moment, second_moment)))
    new_weights, new_master, new_first, new_second = pl.pallas_call(
        functools.partial(apply_kernel, nc, BLOCKS),
        out_shape=(jax.ShapeDtypeStruct((nc, row_dev, dim), bf16),)
        + (jax.ShapeDtypeStruct((row_dev, dim), f32),) * 3,
        in_specs=[smem] + [vmem] * 4,
        out_specs=(hbm,) * 4,
        scratch_shapes=[
            pltpu.VMEM((3, row_dev, dim), f32),
            pltpu.VMEM((row_dev, dim), bf16),
            dma((BLOCKS, 4)), dma((nc - 1,)),
        ],
        compiler_params=pltpu.CompilerParams(vmem_limit_bytes=24 << 20),
        cost_estimate=pl.CostEstimate(
            flops=20 * row_dev * dim, bytes_accessed=40 * row_dev * dim, transcendentals=row_dev * dim
        ),
    )(clip, *(in_vmem(a) for a in kept))
    return (new_weights.reshape(rows, dim), new_master, new_first, new_second)


def solution(mesh):
    in_specs = (
        P(("dp", "ctx"), None),
        P(("dp", "ctx"), "fsdp"),
        P(("fsdp", "ctx"), None),
        P(("fsdp", "ctx"), None),
        P(("fsdp", "ctx"), None),
        P(),
    )
    out_specs = (
        P("fsdp", None),
        P(("fsdp", "ctx"), None),
        P(("fsdp", "ctx"), None),
        P(("fsdp", "ctx"), None),
    )
    return jax.shard_map(
        per_device, mesh=mesh, in_specs=in_specs, out_specs=out_specs, check_vma=False
    )
```

```python
import functools

import jax
import jax.numpy as jnp
from jax import lax
from jax.experimental import pallas as pl
from jax.experimental.pallas import tpu as pltpu
from jax.sharding import PartitionSpec as P

STEP = 10


BETA_ONE = 0.9
BETA_TWO = 0.95
EPSILON = 1e-08
LEARNING_RATE = 0.02
DECAY = 0.1

CHUNKS = 16
BLOCKS = 4
REDUCE = 'NNNNZNNZHHHNNNNN'
GATHER = 'NNNNPNNDGNNGNNDN'
ORDER = (
    0, 1, 2, 3, 4, 5, 6, 16, 17, 7, 8, 18, 9, 19, 22, 21,
    10, 32, 11, 20, 33, 34, 12, 24, 13, 35, 25, 37, 14, 38, 15, 23,
    64, 65, 36, 26, 40, 27, 66, 28, 67, 29, 41, 69, 70, 31, 30, 39,
    68, 96, 56, 43, 97, 42, 44, 98, 57, 45, 99, 47, 71, 101, 72, 84,
    102, 58, 46, 75, 114, 113, 112, 73, 76, 115, 77, 117, 104, 100, 79, 118,
    103, 74, 107, 129, 78, 105, 120, 108, 109, 111, 106, 123, 133, 110, 134, 124,
    121, 116, 125, 130, 127, 122, 131, 136, 142, 140, 128, 137, 141, 132, 135, 139,
    143, 138,
)
MESH = pl.DeviceIdType.MESH


def adamw(grad_sum, master, first_moment, second_moment, clip_scale):
    scaled = clip_scale * grad_sum
    first_new = BETA_ONE * first_moment + (1.0 - BETA_ONE) * scaled
    second_new = BETA_TWO * second_moment + (1.0 - BETA_TWO) * scaled * scaled
    first_hat = first_new / (1.0 - BETA_ONE**STEP)
    second_hat = second_new / (1.0 - BETA_TWO**STEP)
    update = first_hat / (jnp.sqrt(second_hat) + EPSILON)
    fresh_master = master - LEARNING_RATE * (update + DECAY * master)
    return (fresh_master, first_new, second_new)


def reduce_kernel(
    nc, chunks,
    clip_ref, grad_hbm, tok_hbm, master_hbm, first_hbm, second_hbm,
    gathered, master, first, second,
    grad, columns, tok,
    part, part_recv, half_send, half_recv, mid, mid_recv, weights,
    cross_recv, cross_sum, pair_send, pair_recv, quarter_send, quarter_recv, wide_weights, folded,
    grad_sem, tok_sem, state_sem,
    part_ss, part_rs, half_ss, half_rs, mid_ss, mid_rs, near_ss, near_rs,
    own_ss, pass_ss, one_rs, two_rs, far_rs,
    cross_ss, cross_rs, pair_ss, pair_rs,
):
    d = lax.axis_index("dp")
    c = lax.axis_index("ctx")
    x = lax.rem(d, 2)
    y = d // 2
    x_peer = d + 1 - 2 * x
    y_peer = d + 2 - 4 * y
    far_peer = 3 - d
    row_dev, width = weights.shape[1:]
    wide = 4 * width
    half = nc // 2
    hi, lo = c // 2, lax.rem(c, 2)
    pair = c + 1 - 2 * lo
    crossed = [k for k in range(chunks) if REDUCE[k] == "Z"]
    widened = [k for k in range(chunks) if GATHER[k] == "G"]
    bf16, f32 = jnp.bfloat16, jnp.float32

    def place(k):
        return (y, x, y_peer, x_peer) if k % 2 else (x, y, x_peer, y_peer)

    def wide_cols(k):
        return pl.ds(pl.multiple_of(k * wide, 128), wide)

    def cols(k, s):
        return pl.ds(pl.multiple_of(k * wide + s * width, 128), width)

    def tok_copy(k):
        return pltpu.make_async_copy(tok_hbm.at[:, wide_cols(k)], tok.at[:, wide_cols(k)], tok_sem.at[k])

    state_copies = [
        pltpu.make_async_copy(src, dst, state_sem.at[i])
        for i, (src, dst) in enumerate(
            ((master_hbm, master), (first_hbm, first), (second_hbm, second))
        )
    ]

    def block(k, s):
        return gathered.at[:, :, cols(k, s)]

    def send(src, dst, ss, rs, axis, target):
        pltpu.make_async_remote_copy(
            src_ref=src, dst_ref=dst, send_sem=ss, recv_sem=rs,
            device_id={axis: target}, device_id_type=MESH,
        ).start()

    def take(like, sem):
        pltpu.make_async_copy(like, like, sem).wait()

    grad_copy = pltpu.make_async_copy(grad_hbm, grad, grad_sem)
    grad_copy.start()

    @pl.loop(0, chunks)
    def _(k):
        tok_copy(k).start()

    for copy in state_copies:
        copy.start()

    barrier = pltpu.get_barrier_semaphore()
    for peer in (x_peer, y_peer, far_peer):
        pl.semaphore_signal(barrier, inc=1, device_id={"dp": peer}, device_id_type=MESH)
    for j in range(1, nc):
        pl.semaphore_signal(
            barrier, inc=1, device_id={"ctx": lax.rem(c + j, nc)}, device_id_type=MESH
        )
    grad_copy.wait()
    columns[...] = grad[...].T
    pl.semaphore_wait(barrier, nc + 2)

    def others():
        low = (nc - 1 - c) // half
        steps = [j + low * (nc - 2 * j) for j in range(1, nc)]
        return [(j - 1, lax.rem(c + j, nc)) for j in steps]

    def alike():
        return [lax.rem(hi + j, half) for j in range(1, half)]

    def multiply(k):
        one, two, one_peer, _ = place(k)
        tok_copy(k).wait()
        partial = jnp.dot(columns[...], tok[:, wide_cols(k)], preferred_element_type=f32)
        for s in range(4):
            part[k, s // 2, s % 2] = (
                partial[:, s * width:(s + 1) * width].reshape(nc, row_dev, width).astype(bf16)
            )
        if REDUCE[k] != "Z":
            send(part.at[k, 1 - one], part_recv.at[k], part_ss.at[k], part_rs.at[k], "dp", one_peer)
        else:
            z = crossed.index(k)
            for j, to in others():
                send(
                    part.at[k, :, :, to], cross_recv.at[z, j], part_ss.at[k], part_rs.at[k], "ctx", to
                )

    def fold_one(k):
        one, two, one_peer, two_peer = place(k)
        if REDUCE[k] != "Z":
            take(part_recv.at[k], part_rs.at[k])
            half_send[k] = (
                part[k, one, 1 - two].astype(f32) + part_recv[k, 1 - two].astype(f32)
            ).astype(bf16)
            send(half_send.at[k], half_recv.at[k], half_ss.at[k], half_rs.at[k], "dp", two_peer)
        else:
            z = crossed.index(k)
            take(cross_recv.at[z], part_rs.at[k])
            total = part[k, :, :, c].astype(f32)
            for j in range(nc - 1):
                total = total + cross_recv[z, j].astype(f32)
            cross_sum[z] = total
            pair_send[z] = cross_sum[z, 1 - one].astype(bf16)
            send(pair_send.at[z], pair_recv.at[z], half_ss.at[k], half_rs.at[k], "dp", one_peer)

    def fold_two(k):
        one, two, _, two_peer = place(k)
        if REDUCE[k] != "Z":
            take(half_recv.at[k], half_rs.at[k])
            mid[k] = (
                part[k, one, two].astype(f32) + part_recv[k, two].astype(f32)
                + half_recv[k].astype(f32)
            ).astype(bf16).reshape(half, 2, row_dev, width)
            if REDUCE[k] == "H":
                send(
                    mid.at[k, :, 1 - lo], mid_recv.at[k, pl.ds(0, half)],
                    mid_ss.at[k], mid_rs.at[k], "ctx", pair,
                )
            else:
                for j, to in others():
                    send(
                        mid.at[k, to // 2, lax.rem(to, 2)], mid_recv.at[k, j],
                        mid_ss.at[k], mid_rs.at[k], "ctx", to,
                    )
        else:
            z = crossed.index(k)
            take(pair_recv.at[z], half_rs.at[k])
            quarter_send[z] = (
                cross_sum[z, one, 1 - two] + pair_recv[z, 1 - two].astype(f32)
            ).astype(bf16)
            send(quarter_send.at[z], quarter_recv.at[z], mid_ss.at[k], mid_rs.at[k], "dp", two_peer)

    def fold_pair(k):
        take(mid_recv.at[k, pl.ds(0, half)], mid_rs.at[k])
        folded[k] = (
            mid[k, :, lo].astype(f32) + mid_recv[k, pl.ds(0, half)].astype(f32)
        ).astype(bf16)
        for j, to in enumerate(alike()):
            send(
                folded.at[k, to], mid_recv.at[k, half + j],
                cross_ss.at[k], cross_rs.at[k], "ctx", 2 * to + lo,
            )

    def update(k):
        one, two, one_peer, two_peer = place(k)
        here = cols(k, 2 * one + two)
        if REDUCE[k] == "H":
            take(mid_recv.at[k, pl.ds(half, half - 1)], cross_rs.at[k])
            total = mid[k, hi, lo].astype(f32) + mid_recv[k, hi].astype(f32)
            for j in range(half, nc - 1):
                total = total + mid_recv[k, j].astype(f32)
        elif REDUCE[k] == "N":
            take(mid_recv.at[k], mid_rs.at[k])
            total = mid[k, hi, lo].astype(f32)
            for j in range(nc - 1):
                total = total + mid_recv[k, j].astype(f32)
        else:
            z = crossed.index(k)
            take(quarter_recv.at[z], mid_rs.at[k])
            total = (
                cross_sum[z, one, two] + pair_recv[z, two].astype(f32) + quarter_recv[z].astype(f32)
            )
        rounded = total.astype(bf16)
        gathered[c, :, here] = rounded
        if GATHER[k] == "G":
            piece = gathered.at[c, :, here]
            send(piece, piece, own_ss.at[k], one_rs.at[k], "dp", one_peer)
            send(piece, piece, own_ss.at[k], two_rs.at[k], "dp", two_peer)
        else:
            fresh, _, _ = adamw(
                rounded.astype(f32), master[:, here], first[:, here], second[:, here], clip_ref[0]
            )
            weights[k] = fresh.astype(bf16)
            for to in [2 * h + lo for h in alike()] if GATHER[k] in "PQ" else [to for _, to in others()]:
                send(
                    weights.at[k], gathered.at[c, :, here], near_ss.at[k], near_rs.at[k], "ctx", to
                )

    def swap_pair(k):
        one, two, _, _ = place(k)
        here = cols(k, 2 * one + two)
        take(mid_recv.at[k, pl.ds(0, half - 1)], near_rs.at[k])
        send(weights.at[k], gathered.at[c, :, here], pair_ss.at[k], pair_rs.at[k], "ctx", pair)
        for h in alike():
            piece = gathered.at[2 * h + lo, :, here]
            send(piece, piece, pair_ss.at[k], pair_rs.at[k], "ctx", pair)

    def share(k):
        one, two, one_peer, two_peer = place(k)
        s = 2 * one + two
        if GATHER[k] == "G":
            piece = gathered.at[c, :, cols(k, 2 * (1 - one) + two)]
            take(piece, one_rs.at[k])
            send(piece, piece, pass_ss.at[k], far_rs.at[k], "dp", two_peer)
        else:
            if GATHER[k] in "PQ":
                take(mid_recv.at[k, pl.ds(0, half)], pair_rs.at[k])
            else:
                take(mid_recv.at[k], near_rs.at[k])
            send(block(k, s), block(k, s), own_ss.at[k], one_rs.at[k], "dp", one_peer)
            send(block(k, s), block(k, s), own_ss.at[k], two_rs.at[k], "dp", two_peer)
            if GATHER[k] in "DQ":
                send(block(k, s), block(k, s), own_ss.at[k], far_rs.at[k], "dp", far_peer)

    def forward(k):
        one, two, _, two_peer = place(k)
        if GATHER[k] == "G":
            g = widened.index(k)
            piece = weights.at[k]
            take(piece, two_rs.at[k])
            take(piece, far_rs.at[k])
            here = wide_cols(k)
            fresh, _, _ = adamw(
                gathered[c, :, here].astype(f32),
                master[:, here], first[:, here], second[:, here], clip_ref[0],
            )
            wide_weights[g] = fresh.astype(bf16)
            for _, to in others():
                send(
                    wide_weights.at[g], gathered.at[c, :, here], near_ss.at[k], near_rs.at[k],
                    "ctx", to,
                )
        elif GATHER[k] in "NP":
            s = 2 * (1 - one) + two
            take(block(k, s), one_rs.at[k])
            send(block(k, s), block(k, s), pass_ss.at[k], far_rs.at[k], "dp", two_peer)

    def wide_take(k, sem):
        take(gathered.at[pl.ds(0, nc - 1), :, wide_cols(k)], sem)

    def settle(k):
        if GATHER[k] == "G":
            wide_take(k, near_rs.at[k])
        else:
            if GATHER[k] in "DQ":
                take(block(k, 0), one_rs.at[k])
            take(block(k, 0), two_rs.at[k])
            take(block(k, 0), far_rs.at[k])

    stages = (
        multiply, fold_one, fold_two, fold_pair, update, swap_pair, share, forward, settle,
    )
    ready = False
    for entry in ORDER:
        stage, k = divmod(entry, chunks)
        if stage == 4 and not ready:
            for copy in state_copies:
                copy.wait()
            ready = True
        stages[stage](k)

    for k in range(chunks):
        if REDUCE[k] != "Z":
            take(part_recv.at[k], part_ss.at[k])
            take(half_recv.at[k], half_ss.at[k])
            if REDUCE[k] == "H":
                take(mid_recv.at[k, pl.ds(0, half)], mid_ss.at[k])
                take(mid_recv.at[k, pl.ds(half, half - 1)], cross_ss.at[k])
            else:
                take(mid_recv.at[k], mid_ss.at[k])
        else:
            z = crossed.index(k)
            take(cross_recv.at[z], part_ss.at[k])
            take(pair_recv.at[z], half_ss.at[k])
            take(quarter_recv.at[z], mid_ss.at[k])
        if GATHER[k] == "G":
            take(weights.at[pl.ds(0, 2)], own_ss.at[k])
            take(weights.at[k], pass_ss.at[k])
            wide_take(k, near_ss.at[k])
        else:
            if GATHER[k] in "PQ":
                take(mid_recv.at[k, pl.ds(0, half - 1)], near_ss.at[k])
                take(mid_recv.at[k, pl.ds(0, half)], pair_ss.at[k])
            else:
                take(mid_recv.at[k], near_ss.at[k])
            copies = 3 if GATHER[k] in "DQ" else 2
            take(gathered.at[:, :, pl.ds(0, copies * width)], own_ss.at[k])
            if GATHER[k] in "NP":
                take(block(k, 0), pass_ss.at[k])


def apply_kernel(
    nc, blocks,
    clip_ref, gathered, master, first, second,
    weight_out, master_out, first_out, second_out,
    fresh, rounded,
    out_sem, move_sem,
):
    c = lax.axis_index("ctx")
    row_dev, dim = master.shape
    width = dim // blocks
    targets = (master_out, first_out, second_out)

    def cols(k):
        return pl.ds(pl.multiple_of(k * width, 128), width)

    def stores(k):
        return [
            pltpu.make_async_copy(fresh.at[i, :, cols(k)], dst.at[:, cols(k)], out_sem.at[k, i])
            for i, dst in enumerate(targets)
        ] + [
            pltpu.make_async_copy(
                rounded.at[:, cols(k)], weight_out.at[c, :, cols(k)], out_sem.at[k, 3]
            )
        ]

    def move(j):
        row = lax.rem(c + j, nc)
        return pltpu.make_async_copy(gathered.at[row], weight_out.at[row], move_sem.at[j - 1])

    @pl.loop(1, nc)
    def _(j):
        move(j).start()

    @pl.loop(0, blocks)
    def _(k):
        results = adamw(
            gathered[c, :, cols(k)].astype(jnp.float32),
            master[:, cols(k)], first[:, cols(k)], second[:, cols(k)], clip_ref[0],
        )
        for i, value in enumerate(results):
            fresh[i, :, cols(k)] = value
        rounded[:, cols(k)] = results[0].astype(jnp.bfloat16)
        for copy in stores(k):
            copy.start()

    @pl.loop(0, blocks)
    def _(k):
        for copy in stores(k):
            copy.wait()

    @pl.loop(1, nc)
    def _(j):
        move(j).wait()


def per_device(tokens, grad_hidden, master, first_moment, second_moment, clip_scale):
    nc = lax.axis_size("ctx")
    row_dev, dim = master.shape
    tok_rows, rows = grad_hidden.shape
    width = dim // CHUNKS // 4
    crossed = max(1, REDUCE.count("Z"))
    widened = max(1, GATHER.count("G"))
    bf16, f32 = jnp.bfloat16, jnp.float32
    dma = pltpu.SemaphoreType.DMA
    hbm = pl.BlockSpec(memory_space=pl.ANY)
    smem = pl.BlockSpec(memory_space=pltpu.SMEM)
    vmem = pl.BlockSpec(memory_space=pltpu.VMEM)

    def in_hbm(a):
        return pltpu.with_memory_space_constraint(a, pltpu.HBM)

    def in_vmem(a):
        return pltpu.with_memory_space_constraint(a, pltpu.VMEM)

    clip = clip_scale.reshape(1)
    kept = pl.pallas_call(
        functools.partial(reduce_kernel, nc, CHUNKS),
        out_shape=(pltpu.VMEM((nc, row_dev, dim), bf16),) + (pltpu.VMEM((row_dev, dim), f32),) * 3,
        in_specs=[smem] + [hbm] * 5,
        out_specs=(vmem,) * 4,
        scratch_shapes=[
            pltpu.VMEM((tok_rows, rows), bf16),
            pltpu.VMEM((rows, tok_rows), bf16),
            pltpu.VMEM((tok_rows, dim), bf16),
            pltpu.VMEM((CHUNKS, 2, 2, nc, row_dev, width), bf16),
            pltpu.VMEM((CHUNKS, 2, nc, row_dev, width), bf16),
            pltpu.VMEM((CHUNKS, nc, row_dev, width), bf16),
            pltpu.VMEM((CHUNKS, nc, row_dev, width), bf16),
            pltpu.VMEM((CHUNKS, nc // 2, 2, row_dev, width), bf16),
            pltpu.VMEM((CHUNKS, nc - 1, row_dev, width), bf16),
            pltpu.VMEM((CHUNKS, row_dev, width), bf16),
            pltpu.VMEM((crossed, nc - 1, 2, 2, row_dev, width), bf16),
            pltpu.VMEM((crossed, 2, 2, row_dev, width), f32),
            pltpu.VMEM((crossed, 2, row_dev, width), bf16),
            pltpu.VMEM((crossed, 2, row_dev, width), bf16),
            pltpu.VMEM((crossed, row_dev, width), bf16),
            pltpu.VMEM((crossed, row_dev, width), bf16),
            pltpu.VMEM((widened, row_dev, 4 * width), bf16),
            pltpu.VMEM((CHUNKS, nc // 2, row_dev, width), bf16),
            dma, dma((CHUNKS,)), dma((3,)),
        ] + [dma((CHUNKS,))] * 17,
        compiler_params=pltpu.CompilerParams(
            collective_id=0, has_side_effects=True, vmem_limit_bytes=48 << 20
        ),
        cost_estimate=pl.CostEstimate(
            flops=2 * rows * tok_rows * dim,
            bytes_accessed=2 * tok_rows * dim + 4 * rows * dim,
            transcendentals=0,
        ),
    )(clip, *(in_hbm(a) for a in (grad_hidden, tokens, master, first_moment, second_moment)))
    new_weights, new_master, new_first, new_second = pl.pallas_call(
        functools.partial(apply_kernel, nc, BLOCKS),
        out_shape=(jax.ShapeDtypeStruct((nc, row_dev, dim), bf16),)
        + (jax.ShapeDtypeStruct((row_dev, dim), f32),) * 3,
        in_specs=[smem] + [vmem] * 4,
        out_specs=(hbm,) * 4,
        scratch_shapes=[
            pltpu.VMEM((3, row_dev, dim), f32),
            pltpu.VMEM((row_dev, dim), bf16),
            dma((BLOCKS, 4)), dma((nc - 1,)),
        ],
        compiler_params=pltpu.CompilerParams(vmem_limit_bytes=24 << 20),
        cost_estimate=pl.CostEstimate(
            flops=20 * row_dev * dim, bytes_accessed=40 * row_dev * dim, transcendentals=row_dev * dim
        ),
    )(clip, *(in_vmem(a) for a in kept))
    return (new_weights.reshape(rows, dim), new_master, new_first, new_second)


def solution(mesh):
    in_specs = (
        P(("dp", "ctx"), None),
        P(("dp", "ctx"), "fsdp"),
        P(("fsdp", "ctx"), None),
        P(("fsdp", "ctx"), None),
        P(("fsdp", "ctx"), None),
        P(),
    )
    out_specs = (
        P("fsdp", None),
        P(("fsdp", "ctx"), None),
        P(("fsdp", "ctx"), None),
        P(("fsdp", "ctx"), None),
    )
    return jax.shard_map(
        per_device, mesh=mesh, in_specs=in_specs, out_specs=out_specs, check_vma=False
    )
```
